32 devices in a mesh: groups: 2 (over y), ctx: 16 (over z, x, core), dp: 1.
Axes of the slice: x: 2, y: 2, z: 4, core: 2. Of those that a mesh axis runs over, the one named last changes fastest.
Arguments:
- tokens: bfloat16 [4096, 1024], P(('groups', 'ctx', 'dp')), parts along dimension 0, may hold values from -6 to 6
- cotangent: bfloat16 [4096, 1024], P(('groups', 'ctx', 'dp')), parts along dimension 0, may hold values from -6 to 6
- expert_ids: int32 [4096, 8], P(('groups', 'ctx', 'dp')), parts along dimension 0, may hold values from 0 to 15, all different within a row; in each aligned block of 128 rows (0 to 127, 128 to 255, ...) at most 80 rows name the same one
- router_weights: float32 [4096, 8], P(('groups', 'ctx', 'dp')), parts along dimension 0, may hold values from 0.03 to 0.3
- seq_lengths: int32 [8], P('groups'), parts along dimension 0, may hold values from 256 to 768, as said below
- w_gate: bfloat16 [16, 1024, 384], P('ctx', 'dp'), may hold values from -0.1875 to 0.1875
- w_up: bfloat16 [16, 1024, 384], P('ctx', 'dp'), may hold values from -0.1875 to 0.1875
- w_down: bfloat16 [16, 384, 1024], P('ctx', None, 'dp'), may hold values from -0.3125 to 0.3125
Outputs:
- mixed: bfloat16 [4096, 1024], P(('groups', 'ctx', 'dp')), parts along dimension 0
- token_grads: bfloat16 [4096, 1024], P(('groups', 'ctx', 'dp')), parts along dimension 0
- weight_grads: float32 [4096, 8], P(('groups', 'ctx', 'dp')), parts along dimension 0
The draws below stay inside these ranges and needn't reach their ends.
There are 2 independent parts, one for each index of `groups`. The reference program is written for one: setup_inputs(seed, part) draws one part's arguments, and reference() takes and returns one part's arrays. A program takes and returns all parts, laid end to end along the dimension named above; an argument that names none is the same for every part. Nothing has to cross between parts.
Inputs may be any that keep to these rules, and one draw needn't show every extreme that they name: `expert_ids`: in each aligned block of 128 rows (the rows of one device) every expert is named by at most 80 rows, and in every draw some expert is named by exactly 80 rows of some block; the 8 entries of a row differ. `seq_lengths`: the 4 lengths sum to 2048; both ends of the range are reached in every draw.
All inputs are finite; a program needn't handle non-finite values.
Results may differ from the reference program's by a relative error of at most 0.0064.
Values may be sent and summed in bfloat16 or wider, within the bound.
No kernel may reach another device: no remote copies, remote signals or barrier semaphores. Data moves between devices by JAX's collectives and lax.ppermute only.
A program may use at most 128 MiB of HBM per device.

```python
import math
import jax
import jax.numpy as jnp
import numpy as np
from jax import lax

D = 1024
FF = 384
TOPK = 8
TOK_DEV = 128
EXPERTS = 16
CAP = 80
TOKENS = 2048
NSEQ = 4
AVG_LEN = 512


def draw_seq_lengths(key, part):
    half_span = AVG_LEN // 2
    offsets = jax.random.randint(jax.random.fold_in(key, 11), (NSEQ // 2,), 0, half_span + 1)
    offsets = offsets.at[0].set(half_span)
    paired = jnp.stack([AVG_LEN + offsets, AVG_LEN - offsets], axis=1).reshape(NSEQ)
    order = jax.random.permutation(jax.random.fold_in(key, 23), NSEQ)
    return paired[order].astype(jnp.int32)


def shard_levels(own_key, shape, split, least, largest):
    def one(dim, blocks):
        draws = jax.random.uniform(jax.random.fold_in(jax.random.fold_in(own_key, 6), dim), (blocks,), jnp.float32, least / len(split), largest / len(split))
        return jnp.repeat(jnp.exp(draws), shape[dim] // blocks).reshape((-1,) + (1,) * (len(shape) - dim - 1))

    factor_of = one(*split[0])
    for cut in split[1:]:
        factor_of = factor_of * one(*cut)
    return factor_of


def shared_out(stream_key, own, number, rows, number_of, top, limit, skew):
    sequence = jax.random.permutation(stream_key, number_of)
    crowded, usual = portions_of(number_of, rows * top, limit, skew, True), portions_of(number_of, rows * top, limit, skew, False)
    places = jnp.arange(number_of)

    def named(lengths, rotation):
        used = int((lengths > 0).sum())
        fixed = max(1, used // 4)
        shifted = fixed + (places - fixed + rotation * (used - fixed)) % max(1, number_of - fixed)
        return jnp.zeros((number_of,), jnp.int32).at[sequence[jnp.where(places < fixed, places, shifted)]].set(jnp.asarray(lengths, jnp.int32))

    lengths = jnp.where(number % 4 == 0, named(crowded, number // 4), named(usual, number - number // 4 - 1))
    mixed = jax.random.permutation(jax.random.fold_in(own, 3), number_of)
    donor, taker = mixed[0:number_of // 2 * 2:2], mixed[1:number_of // 2 * 2:2]
    margin = jnp.minimum(lengths[donor] - 1, limit - lengths[taker]) // 2
    margin = jnp.where((donor == sequence[0]) | (taker == sequence[0]) | (lengths[taker] == 0), 0, jnp.maximum(margin, 0))
    shifted = jax.random.randint(jax.random.fold_in(own, 4), (number_of // 2,), 0, 1 << 20) % (margin + 1)
    lengths = lengths.at[donor].add(-shifted).at[taker].add(shifted)
    members = jnp.searchsorted(jnp.cumsum(lengths), jnp.arange(rows * top), side="right").astype(jnp.int32)
    table = members.reshape(top, rows).T
    table = table[jax.random.permutation(jax.random.fold_in(own, 1), rows)]
    rotation = jax.random.randint(jax.random.fold_in(own, 2), (rows, 1), 0, top)
    return jnp.take_along_axis(table, (jnp.arange(top)[None, :] + rotation) % top, axis=1)


def portions_of(number_of, total, limit, lean, full):
    weights = [(1 << 20) // math.isqrt(standing ** lean) + 1 for standing in range(1, number_of + 1)]
    largest = limit if full else min(limit, max(-(-total // number_of), total * weights[0] // sum(weights)))
    least = 1 if total - largest >= number_of - 1 else 0
    holding, rest = [largest] + [least] * (number_of - 1), total - largest - least * (number_of - 1)
    while rest > 0:
        movable = [i for i in range(1, number_of) if holding[i] < largest] or [i for i in range(1, number_of) if holding[i] < limit]
        whole, left = sum([weights[i] for i in movable]), rest
        for i in movable:
            addition = min(limit - holding[i], max(1, left * weights[i] // whole), rest)
            holding[i] = holding[i] + addition
            rest = rest - addition
    return np.array(holding)


def normal_values(rng, extent, scale, most, pieces=(), held_as=jnp.bfloat16):
    entries = jax.random.normal(rng, extent, jnp.float32) * scale
    if len(pieces) > 0:
        entries = shard_levels(rng, extent, pieces, -0.22, 0.18) * entries
    return jnp.clip(entries, min=-most, max=most).astype(held_as)


def setup_inputs(seed: int = 0, part: int = 0) -> dict:
    key_list = jax.random.split(jax.random.key(seed), 9)
    part_splits = jax.random.split(jax.random.fold_in(key_list[8], part), 9)
    tokens = normal_values(part_splits[0], (TOKENS, D), 1.0, 6.0, ((0, 16),))
    cotangent = normal_values(part_splits[1], (TOKENS, D), 1.0, 6.0, ((0, 16),))
    expert_ids_keys = jax.random.split(jax.random.fold_in(part_splits[2], 1), TOKENS // TOK_DEV)
    expert_ids_turns = jax.random.permutation(jax.random.fold_in(part_splits[2], 3), TOKENS // TOK_DEV)
    expert_ids = jax.vmap(lambda own, number: shared_out(jax.random.fold_in(part_splits[2], 2), own, number, TOK_DEV, EXPERTS, TOPK, CAP, 2))(expert_ids_keys, expert_ids_turns).reshape((TOKENS, TOPK))
    router_weights = jnp.clip(jnp.exp(math.log(0.3) - 2.3025852 * jax.random.uniform(part_splits[3], (TOKENS, TOPK), jnp.float32) ** shard_levels(part_splits[3], (TOKENS, TOPK), ((0, 16),), -0.2, 0.2)), 0.03, 0.3)
    seq_lengths = draw_seq_lengths(jax.random.fold_in(jax.random.fold_in(key_list[8], part), 71), part)
    w_gate = normal_values(key_list[5], (EXPERTS, D, FF), D ** -0.5, 0.1875, ((0, 16),))
    w_up = normal_values(key_list[6], (EXPERTS, D, FF), D ** -0.5, 0.1875, ((0, 16),))
    w_down = normal_values(key_list[7], (EXPERTS, FF, D), FF ** -0.5, 0.3125, ((0, 16),))
    return {"tokens": tokens, "cotangent": cotangent, "expert_ids": expert_ids, "router_weights": router_weights, "seq_lengths": seq_lengths, "w_gate": w_gate, "w_up": w_up, "w_down": w_down}


def loss_scale(position, seq_lengths, mean_length):
    ends = jnp.cumsum(seq_lengths).astype(jnp.int32)
    starts = ends - seq_lengths
    inside = (position[:, None] >= starts[None, :]) & (position[:, None] < ends[None, :])
    own_length = jnp.sum(jnp.where(inside, seq_lengths[None, :], 0), axis=1)
    return mean_length / own_length.astype(jnp.float32)


def forward_rows(slot_rows, gate_full, up_full, down_full):
    gate_pre = jnp.dot(slot_rows, gate_full, preferred_element_type=jnp.float32)
    up_value = jnp.dot(slot_rows, up_full, preferred_element_type=jnp.float32)
    activated = jax.nn.silu(gate_pre)
    hidden = (activated * up_value).astype(jnp.bfloat16)
    expert_out = jnp.dot(hidden, down_full, preferred_element_type=jnp.float32).astype(jnp.bfloat16)
    return gate_pre, up_value, activated, expert_out


def backward_rows(grad_rows, gate_pre, up_value, activated, gate_full, up_full, down_full):
    contract = (((1,), (1,)), ((), ()))
    hidden_grad = lax.dot_general(grad_rows, down_full, contract, preferred_element_type=jnp.float32)
    sigmoid_value = jax.nn.sigmoid(gate_pre)
    silu_slope = sigmoid_value * (1.0 + gate_pre * (1.0 - sigmoid_value))
    gate_grad = (hidden_grad * up_value * silu_slope).astype(jnp.bfloat16)
    up_grad = (hidden_grad * activated).astype(jnp.bfloat16)
    slot_grad = lax.dot_general(gate_grad, gate_full, contract, preferred_element_type=jnp.float32)
    slot_grad = slot_grad + lax.dot_general(up_grad, up_full, contract, preferred_element_type=jnp.float32)
    return slot_grad.astype(jnp.bfloat16)


def reference(tokens, cotangent, expert_ids, router_weights, seq_lengths, w_gate, w_up, w_down):
    position = jnp.arange(TOKENS, dtype=jnp.int32)
    loss_weight = loss_scale(position, seq_lengths, AVG_LEN * 1.0)
    out_grad = (cotangent.astype(jnp.float32) * loss_weight[:, None]).astype(jnp.bfloat16)
    assign_total = TOKENS * TOPK
    flat_ids = expert_ids.reshape(-1)
    flat_weights = router_weights.reshape(-1)
    slot_total = (TOKENS // TOK_DEV) * CAP

    def per_expert(carry, expert_index):
        mixed_sum, grad_sum, weight_flat = carry
        picked = jnp.nonzero(flat_ids == expert_index, size=slot_total, fill_value=assign_total)[0].astype(jnp.int32)
        filled = picked < assign_total
        clipped = jnp.minimum(picked, assign_total - 1)
        token_of = clipped // TOPK
        slot_rows = jnp.where(filled[:, None], tokens[token_of], jnp.zeros((), jnp.bfloat16))
        grad_rows = jnp.where(filled[:, None], out_grad[token_of], jnp.zeros((), jnp.bfloat16))
        slot_weights = jnp.where(filled, flat_weights[clipped], 0.0)
        gate_full = w_gate[expert_index]
        up_full = w_up[expert_index]
        down_full = w_down[expert_index]
        gate_pre, up_value, activated, expert_out = forward_rows(slot_rows, gate_full, up_full, down_full)
        slot_grad = backward_rows(grad_rows, gate_pre, up_value, activated, gate_full, up_full, down_full)
        mixed_sum = mixed_sum.at[token_of].add(slot_weights[:, None] * expert_out.astype(jnp.float32))
        grad_sum = grad_sum.at[token_of].add(slot_weights[:, None] * slot_grad.astype(jnp.float32))
        inner = jnp.sum(grad_rows.astype(jnp.float32) * expert_out.astype(jnp.float32), axis=1)
        weight_flat = weight_flat.at[picked].set(inner, mode="drop")
        return (mixed_sum, grad_sum, weight_flat), None

    start = (jnp.zeros((TOKENS, D), jnp.float32), jnp.zeros((TOKENS, D), jnp.float32), jnp.zeros((assign_total,), jnp.float32))
    final, _ = lax.scan(per_expert, start, jnp.arange(EXPERTS, dtype=jnp.int32))
    mixed_sum, grad_sum, weight_flat = final
    return mixed_sum.astype(jnp.bfloat16), grad_sum.astype(jnp.bfloat16), weight_flat.reshape(TOKENS, TOPK)
```

```python
import functools

import jax
import jax.numpy as jnp
from jax import lax
from jax.experimental import pallas as pl
from jax.experimental.pallas import tpu as pltpu
from jax.sharding import PartitionSpec as P

LANES = 128
CHUNK = 256
TERMS = 3
CORE_BIT, WEIGHT_BIT, NEAR_BIT, FAR_BIT = 1, 2, 4, 8


def loss_scale(position, seq_lengths, mean_length):
    ends = jnp.cumsum(seq_lengths)
    starts = ends - seq_lengths
    inside = (position[:, None] >= starts[None, :]) & (position[:, None] < ends[None, :])
    own_length = jnp.sum(jnp.where(inside, seq_lengths[None, :], 0), axis=1)
    return mean_length / own_length.astype(jnp.float32)


def forward_rows(slot_rows, gate_full, up_full, down_full):
    gate_pre = jnp.dot(slot_rows, gate_full, preferred_element_type=jnp.float32)
    up_value = jnp.dot(slot_rows, up_full, preferred_element_type=jnp.float32)
    activated = jax.nn.silu(gate_pre)
    hidden = (activated * up_value).astype(jnp.bfloat16)
    expert_out = jnp.dot(hidden, down_full, preferred_element_type=jnp.float32).astype(jnp.bfloat16)
    return (gate_pre, up_value, activated, expert_out)


def backward_rows(grad_rows, gate_pre, up_value, activated, gate_full, up_full, down_full):
    contract = (((1,), (1,)), ((), ()))
    hidden_grad = lax.dot_general(
        grad_rows, down_full, contract, preferred_element_type=jnp.float32
    )
    sigmoid_value = jax.nn.sigmoid(gate_pre)
    silu_slope = sigmoid_value * (1.0 + gate_pre * (1.0 - sigmoid_value))
    gate_grad = (hidden_grad * up_value * silu_slope).astype(jnp.bfloat16)
    up_grad = (hidden_grad * activated).astype(jnp.bfloat16)
    slot_grad = lax.dot_general(gate_grad, gate_full, contract, preferred_element_type=jnp.float32)
    slot_grad = slot_grad + lax.dot_general(
        up_grad, up_full, contract, preferred_element_type=jnp.float32
    )
    return slot_grad.astype(jnp.bfloat16)


def slot_ranks(flat_ids, experts):
    expert_hits = (flat_ids[:, None] == jnp.arange(experts, dtype=jnp.int32)[None, :]).astype(
        jnp.int32
    )
    assign_count = flat_ids.shape[0]
    row_iota = lax.broadcasted_iota(jnp.int32, (assign_count, assign_count), 0)
    col_iota = lax.broadcasted_iota(jnp.int32, (assign_count, assign_count), 1)
    lower_mask = (row_iota > col_iota).astype(jnp.bfloat16)
    earlier = jnp.dot(
        lower_mask, expert_hits.astype(jnp.bfloat16), preferred_element_type=jnp.float32
    )
    return jnp.sum(earlier * expert_hits.astype(jnp.float32), axis=1).astype(jnp.int32)


def per_device_sparse(tokens, cotangent, expert_ids, router_weights, seq_lengths, w_gate, w_up, w_down):
    ctx_count = lax.axis_size("ctx")
    dp_count = lax.axis_size("dp")
    row_count, top_count = expert_ids.shape
    slot_cap = max(2, min(row_count, row_count * top_count * 5 // (4 * ctx_count)))
    block_index = lax.axis_index("ctx") * dp_count + lax.axis_index("dp")
    position = block_index * row_count + jnp.arange(row_count, dtype=jnp.int32)
    loss_weight = loss_scale(position, seq_lengths, row_count * 4.0)
    out_grad = (cotangent.astype(jnp.float32) * loss_weight[:, None]).astype(jnp.bfloat16)
    flat_ids = expert_ids.reshape(-1)
    assign_count = flat_ids.shape[0]
    dest_slot = flat_ids * slot_cap + slot_ranks(flat_ids, ctx_count)
    source_row = jnp.full((ctx_count * slot_cap,), assign_count, jnp.int32)
    source_row = source_row.at[dest_slot].set(jnp.arange(assign_count, dtype=jnp.int32))
    filled = source_row < assign_count
    token_of = jnp.minimum(source_row, assign_count - 1) // top_count
    zero_value = jnp.zeros((), jnp.bfloat16)
    token_send = jnp.where(filled[:, None], tokens[token_of], zero_value).reshape(
        ctx_count, slot_cap, -1
    )
    grad_send = jnp.where(filled[:, None], out_grad[token_of], zero_value).reshape(
        ctx_count, slot_cap, -1
    )
    gate_full, up_full, down_full = (
        lax.all_gather(w_gate[0], "dp", axis=0, tiled=True),
        lax.all_gather(w_up[0], "dp", axis=0, tiled=True),
        lax.all_gather(w_down[0], "dp", axis=1, tiled=True),
    )
    token_arrived = lax.all_to_all(token_send, "ctx", split_axis=0, concat_axis=0, tiled=True)
    grad_arrived = lax.all_to_all(grad_send, "ctx", split_axis=0, concat_axis=0, tiled=True)
    source_count = token_arrived.shape[0]
    slot_count = token_arrived.shape[1]
    slot_rows = token_arrived.reshape(source_count * slot_count, -1)
    grad_rows = grad_arrived.reshape(source_count * slot_count, -1)
    gate_pre, up_value, activated, expert_out = forward_rows(
        slot_rows, gate_full, up_full, down_full
    )
    out_blocks = expert_out.reshape(source_count, slot_count, -1)
    slot_grad = backward_rows(
        grad_rows, gate_pre, up_value, activated, gate_full, up_full, down_full
    )
    out_home = lax.all_to_all(out_blocks, "ctx", split_axis=0, concat_axis=0, tiled=True)
    grad_home = lax.all_to_all(
        slot_grad.reshape(source_count, slot_count, -1),
        "ctx",
        split_axis=0,
        concat_axis=0,
        tiled=True,
    )
    out_rows = out_home.reshape(ctx_count * slot_cap, -1)[dest_slot].reshape(
        row_count, top_count, -1
    )
    grad_rows = grad_home.reshape(ctx_count * slot_cap, -1)[dest_slot].reshape(
        row_count, top_count, -1
    )
    mixed = jnp.sum(router_weights[:, :, None] * out_rows.astype(jnp.float32), axis=1).astype(
        jnp.bfloat16
    )
    token_grads = jnp.sum(
        router_weights[:, :, None] * grad_rows.astype(jnp.float32), axis=1
    ).astype(jnp.bfloat16)
    weight_grads = jnp.einsum("td,tkd->tk", out_grad, out_rows, preferred_element_type=jnp.float32)
    return (mixed, token_grads, weight_grads)


def prep_kernel(mean_length, experts, base_ref, seq_ref, tok_ref, cot_ref, ids_ref, rw_ref, tp_ref, grad_ref):
    rows, width = tok_ref.shape
    position = base_ref[0] + lax.broadcasted_iota(jnp.int32, (rows, 1), 0)
    own_length = jnp.zeros((rows, 1), jnp.int32)
    start = jnp.int32(0)
    for s in range(seq_ref.shape[0]):
        length = seq_ref[s]
        inside = (position >= start) & (position < start + length)
        own_length = jnp.where(inside, length, own_length)
        start = start + length
    loss_weight = mean_length / own_length.astype(jnp.float32)
    grad_ref[...] = (cot_ref[...].astype(jnp.float32) * loss_weight).astype(jnp.bfloat16)
    lane = lax.broadcasted_iota(jnp.int32, (rows, LANES), 1)
    expert = lax.rem(lane, experts)
    dense = jnp.zeros((rows, LANES), jnp.float32)
    for k in range(ids_ref.shape[1]):
        dense = dense + jnp.where(ids_ref[:, k : k + 1] == expert, rw_ref[:, k : k + 1], 0.0)
    high = dense.astype(jnp.bfloat16).astype(jnp.float32)
    middle = (dense - high).astype(jnp.bfloat16).astype(jnp.float32)
    low = dense - high - middle
    packed = jnp.where(lane < experts, high, jnp.where(lane < 2 * experts, middle, low))
    packed = jnp.where(lane < TERMS * experts, packed, 0.0)
    tp_ref[:, :width] = tok_ref[...]
    tp_ref[:, width:] = packed.astype(jnp.bfloat16)


def route_columns(packed, experts, expert_of):
    lane = lax.broadcasted_iota(jnp.int32, packed.shape, 1)
    own = lax.rem(lane, experts)
    wide = packed.astype(jnp.float32)
    return [
        jnp.sum(jnp.where(own == e, wide, 0.0), axis=1, keepdims=True) for e in expert_of
    ]


def start_all(copies):
    for c in copies:
        c.start()


def forward_kernel(experts, count, which_ref, *refs):
    tokens, gates, ups, downs = refs[:4], refs[4 : 4 + count], refs[4 + count : 4 + 2 * count], refs[4 + 2 * count : 4 + 3 * count]
    keep_ref, send_ref, act_ref, slope_ref, hid_ref = refs[4 + 3 * count : 9 + 3 * count]
    x_ref, g_ref, u_ref, d_ref, hw_ref, sem = refs[9 + 3 * count :]
    rows = tokens[0].shape[0]
    width, ff = gates[0].shape
    t_copies = [
        pltpu.make_async_copy(t, x_ref.at[pl.ds(i * rows, rows)], sem.at[i]) for i, t in enumerate(tokens)
    ]
    w_copies = []
    for e in range(count):
        cols = pl.ds(e * ff, ff)
        w_copies.append((
            pltpu.make_async_copy(gates[e], g_ref.at[:, cols], sem.at[4 + 3 * e]),
            pltpu.make_async_copy(ups[e], u_ref.at[:, cols], sem.at[5 + 3 * e]),
            pltpu.make_async_copy(downs[e], d_ref.at[cols, :], sem.at[6 + 3 * e]),
        ))
    start_all(t_copies)
    for e in range(count):
        start_all(w_copies[e][:2])
    for e in range(count):
        w_copies[e][2].start()
    for c in t_copies:
        c.wait()
    scale = route_columns(x_ref[:, width:], experts, [which_ref[e] for e in range(count)])
    x = x_ref[:, :width]
    ready = 0
    for lo in range(0, count * ff, CHUNK):
        while ready < count and ready * ff < lo + CHUNK:
            w_copies[ready][0].wait()
            w_copies[ready][1].wait()
            ready += 1
        gate = jnp.dot(x, g_ref[:, lo : lo + CHUNK], preferred_element_type=jnp.float32)
        up = jnp.dot(x, u_ref[:, lo : lo + CHUNK], preferred_element_type=jnp.float32)
        for j in range(0, CHUNK, LANES):
            cols = slice(lo + j, lo + j + LANES)
            g = gate[:, j : j + LANES]
            u = up[:, j : j + LANES]
            sigmoid = 1.0 / (1.0 + jnp.exp(-g))
            act = g * sigmoid
            hidden = act * u
            act_ref[:, cols] = act.astype(jnp.bfloat16)
            slope_ref[:, cols] = (u * (sigmoid * (1.0 + g * (1.0 - sigmoid)))).astype(jnp.bfloat16)
            hid_ref[:, cols] = hidden.astype(jnp.bfloat16)
            hw_ref[:, cols] = (hidden * scale[(lo + j) // ff]).astype(jnp.bfloat16)
    for e in range(count):
        w_copies[e][2].wait()
    hw = hw_ref[...]
    for lo in range(0, width, CHUNK):
        cols = slice(lo, lo + CHUNK)
        out = jnp.dot(hw, d_ref[:, cols], preferred_element_type=jnp.float32)
        keep_ref[0, :, cols] = out[:rows]
        send_ref[0, :, cols] = out[rows : 2 * rows].astype(jnp.bfloat16)
        keep_ref[1, :, cols] = out[2 * rows : 3 * rows]
        send_ref[1, :, cols] = out[3 * rows :].astype(jnp.bfloat16)


def backward_kernel(experts, count, which_ref, *refs):
    grads, gates, ups, downs = refs[:4], refs[4 : 4 + count], refs[4 + count : 4 + 2 * count], refs[4 + 2 * count : 4 + 3 * count]
    routes = refs[4 + 3 * count : 8 + 3 * count]
    act_ref, slope_ref, hid_ref = refs[8 + 3 * count : 11 + 3 * count]
    keep_ref, send_ref = refs[11 + 3 * count : 13 + 3 * count]
    x_ref, g_ref, u_ref, d_ref, r_ref, gg_ref, ug_ref, sem = refs[13 + 3 * count :]
    rows = grads[0].shape[0]
    width, ff = gates[0].shape
    t_copies = [
        pltpu.make_async_copy(t, x_ref.at[pl.ds(i * rows, rows)], sem.at[i]) for i, t in enumerate(grads)
    ] + [
        pltpu.make_async_copy(t.at[:, pl.ds(width, LANES)], r_ref.at[pl.ds(i * rows, rows)], sem.at[4 + 3 * count + i])
        for i, t in enumerate(routes)
    ]
    w_copies = []
    for e in range(count):
        cols = pl.ds(e * ff, ff)
        w_copies.append((
            pltpu.make_async_copy(gates[e], g_ref.at[:, cols], sem.at[4 + 3 * e]),
            pltpu.make_async_copy(ups[e], u_ref.at[:, cols], sem.at[5 + 3 * e]),
            pltpu.make_async_copy(downs[e], d_ref.at[cols, :], sem.at[6 + 3 * e]),
        ))
    start_all(t_copies)
    for e in range(count):
        w_copies[e][2].start()
    for e in range(count):
        start_all(w_copies[e][:2])
    for c in t_copies:
        c.wait()
    scale = route_columns(r_ref[...], experts, [which_ref[e] for e in range(count)])
    x = x_ref[...]
    contract = (((1,), (1,)), ((), ()))
    inner = [jnp.zeros((4 * rows, LANES), jnp.float32) for _ in range(count)]
    ready = 0
    for lo in range(0, count * ff, CHUNK):
        while ready < count and ready * ff < lo + CHUNK:
            w_copies[ready][2].wait()
            ready += 1
        hidden_grad = lax.dot_general(x, d_ref[lo : lo + CHUNK, :], contract, preferred_element_type=jnp.float32)
        for j in range(0, CHUNK, LANES):
            cols = slice(lo + j, lo + j + LANES)
            e = (lo + j) // ff
            hg = hidden_grad[:, j : j + LANES]
            inner[e] = inner[e] + hg * hid_ref[:, cols].astype(jnp.float32)
            weighted = hg * scale[e]
            gg_ref[:, cols] = (weighted * slope_ref[:, cols].astype(jnp.float32)).astype(jnp.bfloat16)
            ug_ref[:, cols] = (weighted * act_ref[:, cols].astype(jnp.float32)).astype(jnp.bfloat16)
    lane = lax.broadcasted_iota(jnp.int32, (4 * rows, LANES), 1)
    table = jnp.zeros((4 * rows, LANES), jnp.float32)
    own = lax.rem(lane, experts)
    for e in range(count):
        total = jnp.sum(inner[e], axis=1, keepdims=True)
        table = table + jnp.where(own == which_ref[e], total, 0.0)
    high = table.astype(jnp.bfloat16).astype(jnp.float32)
    middle = (table - high).astype(jnp.bfloat16).astype(jnp.float32)
    low = table - high - middle
    packed = jnp.where(lane < experts, high, jnp.where(lane < 2 * experts, middle, low))
    packed = jnp.where(lane < TERMS * experts, packed, 0.0)

    def put(cols, out):
        keep_ref[0, :, cols] = out[:rows]
        send_ref[0, :, cols] = out[rows : 2 * rows].astype(jnp.bfloat16)
        keep_ref[1, :, cols] = out[2 * rows : 3 * rows]
        send_ref[1, :, cols] = out[3 * rows :].astype(jnp.bfloat16)

    put(slice(width, width + LANES), packed)
    for e in range(count):
        w_copies[e][0].wait()
        w_copies[e][1].wait()
    gg = gg_ref[...]
    ug = ug_ref[...]
    for lo in range(0, width, CHUNK):
        out = lax.dot_general(gg, g_ref[lo : lo + CHUNK, :], contract, preferred_element_type=jnp.float32)
        out = out + lax.dot_general(ug, u_ref[lo : lo + CHUNK, :], contract, preferred_element_type=jnp.float32)
        put(slice(lo, lo + CHUNK), out)


def merge_kernel(keep_ref, got_ref, out_ref):
    out_ref[...] = (keep_ref[0] + got_ref[0].astype(jnp.float32)).astype(jnp.bfloat16)


def finish_mixed_kernel(keep_ref, near_ref, far_ref, out_ref):
    total = keep_ref[0] + near_ref[0].astype(jnp.float32) + far_ref[...].astype(jnp.float32)
    out_ref[...] = total.astype(jnp.bfloat16)


def finish_grad_kernel(experts, keep_ref, near_ref, far_ref, ids_ref, out_ref, wg_ref):
    total = keep_ref[0] + near_ref[0].astype(jnp.float32) + far_ref[...].astype(jnp.float32)
    width = out_ref.shape[1]
    out_ref[...] = total[:, :width].astype(jnp.bfloat16)
    table = total[:, width:]
    own = lax.rem(lax.broadcasted_iota(jnp.int32, table.shape, 1), experts)
    picked = [
        jnp.sum(jnp.where(own == ids_ref[:, k : k + 1], table, 0.0), axis=1, keepdims=True)
        for k in range(ids_ref.shape[1])
    ]
    wg_ref[...] = jnp.concatenate(picked, axis=1)


def whole(count=1):
    return [pl.BlockSpec(memory_space=pltpu.VMEM)] * count


def in_place(count=1):
    return [pl.BlockSpec(memory_space=pl.ANY)] * count


def scalars(count=1):
    return [pl.BlockSpec(memory_space=pltpu.SMEM)] * count


def per_device_dense(tokens, cotangent, expert_ids, router_weights, seq_lengths, w_gate, w_up, w_down):
    experts = lax.axis_size("ctx")
    rows, width = tokens.shape
    ff = w_gate.shape[2]
    me = lax.axis_index("ctx")
    bf16, f32 = jnp.bfloat16, jnp.float32
    shape = jax.ShapeDtypeStruct

    def swap(value, bit):
        return lax.ppermute(value, "ctx", [(i, i ^ bit) for i in range(experts)])

    base = (me * rows).astype(jnp.int32).reshape(1)
    mine, grad = pl.pallas_call(
        functools.partial(prep_kernel, rows * 4.0, experts),
        in_specs=scalars(2) + whole(4),
        out_specs=whole(2),
        out_shape=[shape((rows, width + LANES), bf16), shape((rows, width), bf16)],
        name="prep",
    )(base, seq_lengths, tokens, cotangent, expert_ids, router_weights)

    far = swap(mine, FAR_BIT)
    near = swap(mine, NEAR_BIT)
    both = swap(far, NEAR_BIT)
    token_blocks = [mine, near, far, both]
    weights = [w_gate[0], w_up[0], w_down[0]]
    gathered = []
    for w in weights:
        core = swap(w, CORE_BIT)
        other = swap(w, WEIGHT_BIT)
        other_core = swap(other, CORE_BIT)
        gathered.append([w, core, other, other_core])
    count = 4
    which = jnp.stack([me, me ^ CORE_BIT, me ^ WEIGHT_BIT, me ^ (CORE_BIT | WEIGHT_BIT)]).astype(jnp.int32)
    g_far = swap(grad, FAR_BIT)
    g_near = swap(grad, NEAR_BIT)
    g_both = swap(g_far, NEAR_BIT)
    grad_blocks = [grad, g_near, g_far, g_both]
    inner = count * ff
    all_rows = 4 * rows
    weight_scratch = [
        pltpu.VMEM((width, inner), bf16),
        pltpu.VMEM((width, inner), bf16),
        pltpu.VMEM((inner, width), bf16),
    ]
    flops = 2 * all_rows * width * inner * 3
    keep, send, act, slope, hid = pl.pallas_call(
        functools.partial(forward_kernel, experts, count),
        in_specs=scalars(1) + in_place(4 + 3 * count),
        out_specs=whole(5),
        out_shape=[
            shape((2, rows, width), f32),
            shape((2, rows, width), bf16),
            shape((all_rows, inner), bf16),
            shape((all_rows, inner), bf16),
            shape((all_rows, inner), bf16),
        ],
        scratch_shapes=[pltpu.VMEM((all_rows, width + LANES), bf16)] + weight_scratch
        + [pltpu.VMEM((all_rows, inner), bf16), pltpu.SemaphoreType.DMA((4 + 3 * count,))],
        cost_estimate=pl.CostEstimate(flops=flops, bytes_accessed=6 * width * inner + 6 * all_rows * inner, transcendentals=all_rows * inner),
        name="forward",
    )(which, *token_blocks, *gathered[0], *gathered[1], *gathered[2])

    def gather_back(keep, send, tag):
        wide = send.shape[2]
        got = swap(send, NEAR_BIT)
        outgoing = pl.pallas_call(
            merge_kernel,
            grid=(1,),
            in_specs=[
                pl.BlockSpec((1, rows, wide), lambda i: (1, 0, 0)),
                pl.BlockSpec((1, rows, wide), lambda i: (1, 0, 0)),
            ],
            out_specs=pl.BlockSpec((rows, wide), lambda i: (0, 0)),
            out_shape=shape((rows, wide), bf16),
            name="merge_" + tag,
        )(keep, got)
        return got, swap(outgoing, FAR_BIT)

    got, came = gather_back(keep, send, "mixed")
    g_keep, g_send = pl.pallas_call(
        functools.partial(backward_kernel, experts, count),
        in_specs=scalars(1) + in_place(8 + 3 * count) + whole(3),
        out_specs=whole(2),
        out_shape=[shape((2, rows, width + LANES), f32), shape((2, rows, width + LANES), bf16)],
        scratch_shapes=[pltpu.VMEM((all_rows, width), bf16)] + weight_scratch
        + [
            pltpu.VMEM((all_rows, LANES), bf16),
            pltpu.VMEM((all_rows, inner), bf16),
            pltpu.VMEM((all_rows, inner), bf16),
            pltpu.SemaphoreType.DMA((8 + 3 * count,)),
        ],
        cost_estimate=pl.CostEstimate(flops=flops, bytes_accessed=6 * width * inner + 6 * all_rows * inner, transcendentals=0),
        name="backward",
    )(which, *grad_blocks, *gathered[0], *gathered[1], *gathered[2], *token_blocks, act, slope, hid)
    g_got, g_came = gather_back(g_keep, g_send, "grad")

    def first(wide):
        return pl.BlockSpec((1, rows, wide), lambda i: (0, 0, 0))

    def flat(wide):
        return pl.BlockSpec((rows, wide), lambda i: (0, 0))

    mixed = pl.pallas_call(
        finish_mixed_kernel,
        grid=(1,),
        in_specs=[first(width), first(width), flat(width)],
        out_specs=flat(width),
        out_shape=shape((rows, width), bf16),
        name="finish_mixed",
    )(keep, got, came)
    top = expert_ids.shape[1]
    token_grads, weight_grads = pl.pallas_call(
        functools.partial(finish_grad_kernel, experts),
        grid=(1,),
        in_specs=[first(width + LANES), first(width + LANES), flat(width + LANES), flat(top)],
        out_specs=[flat(width), flat(top)],
        out_shape=[shape((rows, width), bf16), shape((rows, top), f32)],
        name="finish_grad",
    )(g_keep, g_got, g_came, expert_ids)
    return mixed, token_grads, weight_grads


def spread_fits(mesh, args):
    tokens, expert_ids, w_gate = args[0], args[2], args[5]
    ctx = mesh.shape["ctx"]
    ff = w_gate.shape[2]
    block = tokens.shape[0] // (mesh.shape["groups"] * ctx * mesh.shape["dp"])
    return (
        mesh.shape["dp"] == 1
        and w_gate.shape[0] == ctx
        and ctx == 2 * FAR_BIT
        and expert_ids.shape[1] * 2 >= ctx
        and TERMS * ctx <= LANES
        and tokens.shape[1] % CHUNK == 0
        and ff % LANES == 0
        and (4 * ff) % CHUNK == 0
        and block % 16 == 0
    )


def solution(mesh):
    in_specs = (
        P(("groups", "ctx", "dp"), None),
        P(("groups", "ctx", "dp"), None),
        P(("groups", "ctx", "dp"), None),
        P(("groups", "ctx", "dp"), None),
        P("groups"),
        P("ctx", "dp", None),
        P("ctx", "dp", None),
        P("ctx", None, "dp"),
    )
    out_specs = (
        P(("groups", "ctx", "dp"), None),
        P(("groups", "ctx", "dp"), None),
        P(("groups", "ctx", "dp"), None),
    )

    def step(*args):
        per_device = per_device_dense if spread_fits(mesh, args) else per_device_sparse
        return jax.shard_map(
            per_device, mesh=mesh, in_specs=in_specs, out_specs=out_specs, check_vma=False
        )(*args)

    return step
```
